128 devices in a mesh: head: 8 (over z_hi, x), frame: 16 (over z_lo, y, core).
Axes of the slice: x: 4, y: 4, z: 4 (z_hi: 2, z_lo: 2; z = z_hi * 2 + z_lo), core: 2. Of those that a mesh axis runs over, the one named last changes fastest.
Arguments:
- query_tok: bfloat16 [12288, 3072], P('frame', 'head'), may hold values from -200 to 200
- key_tok: bfloat16 [12288, 3072], P('frame', 'head'), may hold values from -8 to 8
- value_tok: bfloat16 [12288, 3072], P('frame', 'head'), may hold values from -6 to 6
- head_span: int32 [24], P('head'), may hold values from 0 to 3
- out_weight: bfloat16 [3072, 3072], P('head'), may hold values from -0.109375 to 0.109375
Outputs:
- projected: bfloat16 [12288, 3072], P('frame', 'head')
The draws below stay inside these ranges and needn't reach their ends.
All inputs are finite; a program needn't handle non-finite values.
Results may differ from the reference program's by a relative error of at most 0.012.
Values may be sent and summed in bfloat16 or wider, within the bound.
A program may use at most 64 MiB of HBM per device.

```python
import jax
import jax.numpy as jnp
from jax import lax

HEADS = 24
HD = 128
D = 3072
FRAME_TOK = 384
FRAMES = 32
TOKENS = 12288
N_HEAD = 8


def shared_keys(key):
    return jnp.clip(jax.random.normal(jax.random.fold_in(key, 11), (TOKENS, HEADS * HD), jnp.float32), -8.0, 8.0)


def draw_key_tok(key, part):
    return shared_keys(key).astype(jnp.bfloat16)


def draw_query_tok(key, part):
    base = jnp.clip(jax.random.normal(jax.random.fold_in(key, 12), (TOKENS, HEADS * HD), jnp.float32), -6.0, 6.0)
    return base.astype(jnp.bfloat16)


def touch_ends(entries, own_key, smallest, largest):
    spot = [jax.random.randint(jax.random.fold_in(own_key, axis), (), 0, length) for axis, length in enumerate(entries.shape)]
    widest = entries.shape.index(max(entries.shape))
    next_to = spot[:widest] + [(spot[widest] + 1) % entries.shape[widest]] + spot[widest + 1:]
    return entries.at[tuple(spot)].set(smallest).at[tuple(next_to)].set(largest)


def block_scale(rng, shape, shards, smallest, largest):
    def one(dim, parts):
        steps = jax.random.uniform(jax.random.fold_in(jax.random.fold_in(rng, 6), dim), (parts,), jnp.float32, smallest / len(shards), largest / len(shards))
        return jnp.repeat(jnp.exp(steps), shape[dim] // parts).reshape((-1,) + (1,) * (len(shape) - dim - 1))

    loudness = one(*shards[0])
    for cut in shards[1:]:
        loudness = loudness * one(*cut)
    return loudness


def noise(stream_key, dims, spread, bound, split=(), kind=jnp.bfloat16):
    factor_of = block_scale(stream_key, dims, split, -0.22, 0.18) if split else 1.0
    values = jax.random.normal(stream_key, dims, jnp.float32) * spread * factor_of
    return jnp.minimum(jnp.maximum(values, -bound), bound).astype(kind)


def setup_inputs(seed: int = 0) -> dict:
    key_list = jax.random.split(jax.random.key(seed), 6)
    query_tok = draw_query_tok(jax.random.fold_in(key_list[5], 71), 0)
    key_tok = draw_key_tok(jax.random.fold_in(key_list[5], 71), 0)
    value_tok = noise(key_list[2], (TOKENS, HEADS * HD), 1.0, 6.0, ((0, 16), (1, 8)))
    head_span = touch_ends(jax.random.randint(key_list[3], (HEADS,), 0, 4), jax.random.fold_in(key_list[3], 1), 0, 3).astype(jnp.int32)
    out_weight = noise(key_list[4], (HEADS * HD, D), (HEADS * HD) ** -0.5, 0.109375, ((0, 8),))
    return dict(query_tok=query_tok, key_tok=key_tok, value_tok=value_tok, head_span=head_span, out_weight=out_weight)


def attend(query_frame, key_rows, value_rows, frame_pos, head_span):
    scale = 1.0 / (HD ** 0.5)
    scores = jnp.einsum("qhd,khd->hqk", query_frame.astype(jnp.float32), key_rows.astype(jnp.float32)) * scale
    offsets = jnp.arange(7, dtype=jnp.int32) - 3
    allowed = (jnp.abs(offsets)[None, :] <= head_span[:, None]) & (frame_pos + offsets >= 0)[None, :] & (frame_pos + offsets < FRAMES)[None, :]
    visible = jnp.repeat(allowed, FRAME_TOK, axis=1)[:, None, :]
    scores = jnp.where(visible, scores, -1e30)
    rowmax = jnp.max(scores, axis=2, keepdims=True)
    weights = jnp.where(visible, jnp.exp(scores - rowmax), 0.0)
    total = jnp.sum(weights, axis=2)
    probs = weights.astype(jnp.bfloat16)
    mixed = jnp.einsum("hqk,khd->qhd", probs.astype(jnp.float32), value_rows.astype(jnp.float32))
    return (mixed / jnp.transpose(total)[:, :, None]).astype(jnp.bfloat16)


def reference(query_tok, key_tok, value_tok, head_span, out_weight):
    query_all = query_tok.reshape(FRAMES, FRAME_TOK, HEADS, HD)
    widths = ((3, 3), (0, 0), (0, 0), (0, 0))
    key_pad = jnp.pad(key_tok.reshape(FRAMES, FRAME_TOK, HEADS, HD), widths)
    value_pad = jnp.pad(value_tok.reshape(FRAMES, FRAME_TOK, HEADS, HD), widths)

    def one_frame(frame_pos):
        key_rows = lax.dynamic_slice_in_dim(key_pad, frame_pos, 7, 0).reshape(7 * FRAME_TOK, HEADS, HD)
        value_rows = lax.dynamic_slice_in_dim(value_pad, frame_pos, 7, 0).reshape(7 * FRAME_TOK, HEADS, HD)
        query_frame = lax.dynamic_index_in_dim(query_all, frame_pos, 0, keepdims=False)
        return attend(query_frame, key_rows, value_rows, frame_pos, head_span)

    attended = lax.map(one_frame, jnp.arange(FRAMES, dtype=jnp.int32)).reshape(TOKENS, HEADS * HD)
    group = HEADS * HD // N_HEAD
    summed = jnp.zeros((TOKENS, D), jnp.float32)
    for index in range(N_HEAD):
        partial_value = jnp.dot(attended[:, index * group:(index + 1) * group], out_weight[index * group:(index + 1) * group], preferred_element_type=jnp.float32).astype(jnp.bfloat16)
        partial_value = lax.optimization_barrier(partial_value)
        summed = summed + partial_value.astype(jnp.float32)
    return summed.astype(jnp.bfloat16)
```

```python
import functools
import math

import jax
import jax.numpy as jnp
from jax import lax
from jax.experimental import pallas as pl
from jax.experimental.pallas import tpu as pltpu
from jax.sharding import PartitionSpec as P

MESH = pl.DeviceIdType.MESH
HD = 128
T = 384
HALF = T // 2
G = 384
NH = 3
NX = 4
F32 = jnp.float32
BF16 = jnp.bfloat16
SCALE = math.log2(math.e) / math.sqrt(HD)
HIDDEN = -1e30


def kernel(
    span_ref, q_hbm, k_hbm, v_hbm, w_hbm, o_ref,
    qv, kw, vw, w_own, w_oth, acc, top, att, att_oth, pb, own, keep, relay, comb, final,
    lsem, hs, hr, ws, wr, zs, zr, xs, xr,
):
    head = lax.axis_index("head")
    frame = lax.axis_index("frame")
    frames = lax.axis_size("frame")
    zh, x = head // NX, head % NX
    core = frame % 2
    step = 1 - 2 * core
    sib = (head, frame + step)
    far = (head, frame - step)
    over = (head, frame + 2 * step)
    under = (head, frame - 2 * step)
    last = frames - 1
    far_ok = (frame - step >= 0) & (frame - step <= last)
    over_ok = (frame + 2 * step >= 0) & (frame + 2 * step <= last)
    zpart = ((1 - zh) * NX + x, frame)
    znear = ((1 - zh) * NX + x, (frame + frames // 2) % frames)
    right = (zh * NX + (x + 1) % NX, frame)
    left = (zh * NX + (x + NX - 1) % NX, frame)

    def rows(i):
        return pl.ds(pl.multiple_of((core + i) % 2 * T, T), T)

    def local(src, dst, n):
        copy = pltpu.make_async_copy(src, dst, lsem.at[n])
        copy.start()
        return copy

    def remote(src, dst, send, recv, device):
        return pltpu.make_async_remote_copy(
            src_ref=src, dst_ref=dst, send_sem=send, recv_sem=recv, device_id=device, device_id_type=MESH
        )

    q_in = [local(q_hbm.at[rows(i), :], qv.at[i], i) for i in range(2)]
    kv_in = [local(k_hbm.at[rows(i), :], kw.at[3 + i], 2 + i) for i in range(2)]
    kv_in += [local(v_hbm.at[rows(i), :], vw.at[3 + i], 4 + i) for i in range(2)]

    barrier = pltpu.get_barrier_semaphore()

    def greet(device):
        pl.semaphore_signal(barrier, inc=1, device_id=device, device_id_type=MESH)

    for device in (sib, zpart, znear, right, left):
        greet(device)

    @pl.when(far_ok)
    def _():
        greet(far)
        greet(under)

    @pl.when(over_ok)
    def _():
        greet(over)

    pl.semaphore_wait(barrier, 5 + 2 * far_ok.astype(jnp.int32) + over_ok.astype(jnp.int32))

    def halo(i, slot, device):
        return [
            remote(src.at[rows(i), :], dst.at[slot], hs.at[n, slot], hr.at[n, slot], device)
            for n, (src, dst) in enumerate(((k_hbm, kw), (v_hbm, vw)))
        ]

    to_far = [halo(0, 2, far), halo(1, 1, far)]
    to_sib = [halo(1, 5, sib), halo(0, 6, sib)]
    to_over = halo(1, 0, over)
    forward = [
        remote(buf.at[2], buf.at[7], hs.at[n, 7], hr.at[n, 7], sib) for n, buf in enumerate((kw, vw))
    ]

    @pl.when(far_ok)
    def _():
        for copy in to_far[0]:
            copy.start()

    for pair in to_sib:
        for copy in pair:
            copy.start()

    mine = pl.ds(pl.multiple_of(core * HALF, HALF), HALF)

    def columns(group, d):
        return pl.ds(pl.multiple_of(group * (NX * G) + d * G, G), G)

    w_near = [
        remote(w_hbm.at[mine, columns(1 - zh, d)], w_oth.at[d, mine, :], ws.at[d], wr.at[d], znear) for d in range(NX)
    ]
    w_pass = remote(w_oth.at[:, mine, :], w_oth.at[:, mine, :], ws.at[NX], wr.at[NX], sib)
    for copy in w_near:
        copy.start()
    w_in = [local(w_hbm.at[:, columns(zh, d)], w_own.at[d], 6 + d) for d in range(NX)]

    for copy in q_in + kv_in:
        copy.wait()

    def attend(i, hd, slots, first=False):
        cols = slice(hd * HD, (hd + 1) * HD)
        n = len(slots)
        query = qv[i, :, cols]
        keys = kw[slots[0] : slots[0] + n, :, cols].reshape(n * T, HD)
        values = vw[slots[0] : slots[0] + n, :, cols].reshape(n * T, HD)
        s = lax.dot_general(query, keys, (((1,), (1,)), ((), ())), preferred_element_type=F32) * SCALE
        span = span_ref[hd]
        bias = [jnp.where(jnp.abs(3 + i - slot) <= span, 0.0, HIDDEN).astype(F32) for slot in slots]
        new = None
        for b, part in zip(bias, [s[:, m * T : (m + 1) * T] for m in range(n)]):
            peak = jnp.max(part, axis=1, keepdims=True) + b
            new = peak if new is None else jnp.maximum(new, peak)
        new = jnp.broadcast_to(new, (T, HD))
        if not first:
            old = top[i, hd]
            new = jnp.maximum(old, new)
            shrink = jnp.exp2(old - new)
        shift = jnp.concatenate([new - b for b in bias for _ in range(T // HD)], axis=1)
        p = jnp.exp2(s - shift).astype(BF16)
        extended = jnp.concatenate([values, jnp.ones((n * T, HD), BF16)], axis=1)
        out = jnp.dot(p, extended, preferred_element_type=F32)
        top[i, hd] = new
        if first:
            acc[i, hd] = out
        else:
            acc[i, hd] = acc[i, hd] * jnp.concatenate([shrink, shrink], axis=1) + out

    def attend_both(slots, first=False):
        @pl.loop(0, 2)
        def _(i):
            for hd in range(NH):
                attend(i, hd, slots, first)

    def finish(i):
        for hd in range(NH):
            att[i, :, hd * HD : (hd + 1) * HD] = (acc[i, hd, :, :HD] / acc[i, hd, :, HD:]).astype(BF16)

    attend_both((3, 4), first=True)
    for pair in to_sib:
        for copy in pair:
            copy.wait_recv()
    attend_both((5, 6))

    @pl.when(far_ok)
    def _():
        for copy in to_far[0]:
            copy.wait_send()
        for copy in to_far[1]:
            copy.start()
        for copy in to_far[0]:
            copy.wait_recv()
        for copy in forward:
            copy.start()
        attend_both((2,))

    @pl.when(over_ok)
    def _():
        for copy in forward:
            copy.wait_recv()
        for hd in range(NH):
            attend(1, hd, (7,))

    @pl.when(far_ok)
    def _():
        for copy in to_far[1]:
            copy.wait_send()

    @pl.when(over_ok)
    def _():
        for copy in to_over:
            copy.start()

    @pl.when(far_ok)
    def _():
        for copy in to_far[1]:
            copy.wait_recv()
        attend_both((1,))

    to_z = [remote(att.at[i], att_oth.at[i], zs.at[i], zr.at[i], zpart) for i in range(2)]
    finish(1)
    to_z[1].start()
    for copy in w_near:
        copy.wait_recv()
    w_pass.start()
    for copy in w_in:
        copy.wait()

    @pl.when(far_ok)
    def _():
        for copy in to_over:
            copy.wait_recv()
        for hd in range(NH):
            attend(0, hd, (0,))

    finish(0)
    to_z[0].start()
    w_pass.wait_recv()

    lo, hi = pl.ds(0, HALF), pl.ds(HALF, HALF)

    def shift_x(i):
        def send(n, src, dst, device):
            return remote(src, dst, xs.at[i, n], xr.at[i, n], device)

        return [
            send(0, pb.at[i, 0, lo, :], relay.at[i, 0], right),
            send(1, pb.at[i, 0, hi, :], relay.at[i, 1], left),
            send(2, pb.at[i, 1, hi, :], final.at[i, 1], right),
            send(3, pb.at[i, 2, lo, :], final.at[i, 3], left),
            send(4, comb.at[i, 0], final.at[i, 0], right),
            send(5, comb.at[i, 1], final.at[i, 2], left),
        ]

    moves = [shift_x(i) for i in range(2)]

    def project(i):
        to_z[i].wait_recv()
        both = jnp.concatenate([att[i], att_oth[i]], axis=1)

        def block(r):
            d = (x + r) % NX
            return jnp.dot(both, jnp.concatenate([w_own[d], w_oth[d]], axis=0), preferred_element_type=F32)

        pb[i, 0] = block(2).astype(BF16)
        moves[i][0].start()
        moves[i][1].start()
        part = block(1)
        keep[i, 0] = part[:HALF]
        pb[i, 1, HALF:, :] = part[HALF:].astype(BF16)
        moves[i][2].start()
        part = block(3)
        keep[i, 1] = part[HALF:]
        pb[i, 2, :HALF, :] = part[:HALF].astype(BF16)
        moves[i][3].start()
        own[i] = block(0)

    def combine(i):
        for n in range(2):
            moves[i][n].wait_recv()
            comb[i, n] = (keep[i, n] + relay[i, n].astype(F32)).astype(BF16)
            moves[i][4 + n].start()

    def collect(i):
        for n in range(2, 6):
            moves[i][n].wait_recv()
        block = (core + i) % 2
        o_ref[block, :HALF, :] = (
            own[i, :HALF] + final[i, 0].astype(F32) + final[i, 3].astype(F32)
        ).astype(BF16)
        o_ref[block, HALF:, :] = (
            own[i, HALF:] + final[i, 1].astype(F32) + final[i, 2].astype(F32)
        ).astype(BF16)

    project(1)
    combine(1)
    project(0)
    combine(0)
    collect(1)
    collect(0)

    for pair in to_sib:
        for copy in pair:
            copy.wait_send()

    @pl.when(far_ok)
    def _():
        for copy in forward:
            copy.wait_send()

    @pl.when(over_ok)
    def _():
        for copy in to_over:
            copy.wait_send()

    for copy in w_near:
        copy.wait_send()
    w_pass.wait_send()
    for i in range(2):
        to_z[i].wait_send()
        for copy in moves[i]:
            copy.wait_send()


def body(query_tok, key_tok, value_tok, head_span, out_weight):
    anywhere = pl.BlockSpec(memory_space=pl.ANY)
    dma = pltpu.SemaphoreType.DMA
    out = pl.pallas_call(
        kernel,
        name="window_attention",
        out_shape=jax.ShapeDtypeStruct((2, T, G), BF16),
        in_specs=[pl.BlockSpec(memory_space=pltpu.SMEM)] + [anywhere] * 4,
        out_specs=pl.BlockSpec(memory_space=pltpu.VMEM),
        scratch_shapes=[
            pltpu.VMEM((2, T, G), BF16),
            pltpu.VMEM((8, T, G), BF16),
            pltpu.VMEM((8, T, G), BF16),
            pltpu.VMEM((NX, G, G), BF16),
            pltpu.VMEM((NX, G, G), BF16),
            pltpu.VMEM((2, NH, T, 2 * HD), F32),
            pltpu.VMEM((2, NH, T, HD), F32),
            pltpu.VMEM((2, T, G), BF16),
            pltpu.VMEM((2, T, G), BF16),
            pltpu.VMEM((2, 3, T, G), BF16),
            pltpu.VMEM((2, T, G), F32),
            pltpu.VMEM((2, 2, HALF, G), F32),
            pltpu.VMEM((2, 2, HALF, G), BF16),
            pltpu.VMEM((2, 2, HALF, G), BF16),
            pltpu.VMEM((2, 4, HALF, G), BF16),
            dma((10,)),
            dma((2, 8)),
            dma((2, 8)),
            dma((NX + 1,)),
            dma((NX + 1,)),
            dma((2,)),
            dma((2,)),
            dma((2, 6)),
            dma((2, 6)),
        ],
        compiler_params=pltpu.CompilerParams(
            collective_id=0, has_side_effects=True, vmem_limit_bytes=56 * 1024 * 1024
        ),
    )(head_span, query_tok, key_tok, value_tok, out_weight)
    return out.reshape(2 * T, G)


def solution(mesh):
    return jax.shard_map(
        body,
        mesh=mesh,
        in_specs=(
            P("frame", "head"),
            P("frame", "head"),
            P("frame", "head"),
            P("head"),
            P("head", None),
        ),
        out_specs=P("frame", "head"),
        check_vma=False,
    )
```

```python
import math

import jax
import jax.numpy as jnp
from jax import lax
from jax.experimental import pallas as pl
from jax.experimental.pallas import tpu as pltpu
from jax.sharding import PartitionSpec as P

MESH = pl.DeviceIdType.MESH
HD = 128
T = 384
HALF = T // 2
G = 384
NH = 3
NX = 4
F32 = jnp.float32
BF16 = jnp.bfloat16
SCALE = math.log2(math.e) / math.sqrt(HD)
HIDDEN = -1e30


def kernel(
    span_ref, q_hbm, k_hbm, v_hbm, w_hbm, o_ref,
    qv, kv, wb, acc, top, att, pz, own, got,
    lsem, hs, hr, es, er, ws, wr, xs, xr, rs, rr, zs, zr,
):
    head = lax.axis_index("head")
    frame = lax.axis_index("frame")
    frames = lax.axis_size("frame")
    zh, x = head // NX, head % NX
    core = frame % 2
    step = 1 - 2 * core
    sib = (head, frame + step)
    far = (head, frame - step)
    over = (head, frame + 2 * step)
    under = (head, frame - 2 * step)
    last = frames - 1
    far_ok = (frame - step >= 0) & (frame - step <= last)
    over_ok = (frame + 2 * step >= 0) & (frame + 2 * step <= last)
    zpart = ((1 - zh) * NX + x, frame)
    right = (zh * NX + (x + 1) % NX, frame)
    left = (zh * NX + (x + NX - 1) % NX, frame)
    across = (zh * NX + (x + 2) % NX, frame)

    def rows(i):
        return pl.ds(pl.multiple_of((core + i) % 2 * T, T), T)

    def columns(g, d):
        group = zh if g else 1 - zh
        return pl.ds(pl.multiple_of((group * NX + d) * G, G), G)

    def local(src, dst, n):
        copy = pltpu.make_async_copy(src, dst, lsem.at[n])
        copy.start()
        return copy

    def remote(src, dst, send, recv, device):
        return pltpu.make_async_remote_copy(
            src_ref=src, dst_ref=dst, send_sem=send, recv_sem=recv, device_id=device, device_id_type=MESH
        )

    own_in, n = [], 0
    for i in range(2):
        for hd in range(NH):
            cols = pl.ds(hd * HD, HD)
            own_in.append(local(k_hbm.at[rows(i), cols], kv.at[3 + i, hd, 0], n))
            own_in.append(local(v_hbm.at[rows(i), cols], kv.at[3 + i, hd, 1], n + 1))
            own_in.append(local(q_hbm.at[rows(i), cols], qv.at[i, hd], n + 2))
            n += 3
    w_in = [local(w_hbm.at[:, columns(g, x)], wb.at[g, 0], n + g) for g in range(2)]

    barrier = pltpu.get_barrier_semaphore()

    def greet(device):
        pl.semaphore_signal(barrier, inc=1, device_id=device, device_id_type=MESH)

    for device in (sib, zpart, right, left, across):
        greet(device)

    @pl.when(far_ok)
    def _():
        greet(far)
        greet(under)

    @pl.when(over_ok)
    def _():
        greet(over)

    for copy in own_in:
        copy.wait()
    pl.semaphore_wait(barrier, 5 + 2 * far_ok.astype(jnp.int32) + over_ok.astype(jnp.int32))

    def halo(src, dst, device, hd):
        return remote(kv.at[src, hd], kv.at[dst, hd], hs.at[dst, hd], hr.at[dst, hd], device)

    def to_far(hd):
        return halo(3, 2, far, hd)

    def to_sib(src, hd):
        return halo(src, 9 - src, sib, hd)

    def to_over(hd):
        return halo(5, 1, over, hd)

    def forward(hd):
        return halo(2, 7, sib, hd)

    def edge_keys(hd):
        return remote(kv.at[4, hd, 0], kv.at[0, hd, 0], es.at[0, hd], er.at[0, hd], over)

    def edge_values(hd):
        return remote(kv.at[5, hd, 1], kv.at[0, hd, 1], es.at[1, hd], er.at[1, hd], far)

    def each(*actions):
        @pl.loop(0, NH)
        def _(hd):
            for action in actions:
                action(hd)

    @pl.when(far_ok)
    def _():
        each(lambda hd: to_far(hd).start())

    each(lambda hd: to_sib(4, hd).start())
    each(lambda hd: to_sib(3, hd).start())

    mine = pl.ds(pl.multiple_of(core * HALF, HALF), HALF)
    w_out = [
        remote(w_hbm.at[mine, columns(g, (x + r) % NX)], wb.at[g, NX - r, mine, :], ws.at[r - 1, g], wr.at[r - 1, g], device)
        for r, device in ((2, across), (1, right), (3, left))
        for g in range(2)
    ]
    w_pass = [
        remote(wb.at[:, r, mine, :], wb.at[:, r, mine, :], ws.at[NX - 2 + r, 0], wr.at[NX - 2 + r, 0], sib)
        for r in range(1, NX)
    ]
    for copy in w_out:
        copy.start()

    def attend(i, hd, slot, n, first=False):
        keys = kv[slot : slot + n, hd, 0].reshape(n * T, HD)
        values = kv[slot : slot + n, hd, 1].reshape(n * T, HD)
        s = lax.dot_general(qv[i, hd], keys, (((1,), (1,)), ((), ())), preferred_element_type=F32) * SCALE
        span = span_ref[hd]
        bias = [jnp.where(jnp.abs(3 + i - slot - m) <= span, 0.0, HIDDEN).astype(F32) for m in range(n)]
        new = None
        for m in range(n):
            peak = jnp.max(s[:, m * T : (m + 1) * T], axis=1, keepdims=True) + bias[m]
            new = peak if new is None else jnp.maximum(new, peak)
        new = jnp.broadcast_to(new, (T, HD))
        if not first:
            old = top[i, hd]
            new = jnp.maximum(old, new)
            shrink = jnp.exp2(old - new)
        shift = jnp.concatenate([new - b for b in bias for _ in range(T // HD)], axis=1)
        p = jnp.exp2(s - shift).astype(BF16)
        extended = jnp.concatenate([values, jnp.ones((n * T, HD), BF16)], axis=1)
        out = jnp.dot(p, extended, preferred_element_type=F32)
        top[i, hd] = new
        if first:
            acc[i, hd] = out
        else:
            acc[i, hd] = acc[i, hd] * jnp.concatenate([shrink, shrink], axis=1) + out

    def attend_both(slot, n, first=False):
        @pl.loop(0, 2 * NH)
        def _(u):
            attend(u // NH, u % NH, slot, n, first)

    def to_right(i, hd):
        return remote(att.at[i, 0, hd], att.at[i, 3, hd], xs.at[i, 0, hd], xr.at[i, 0, hd], right)

    def to_left(i, hd):
        return remote(att.at[i, 0, hd], att.at[i, 1, hd], xs.at[i, 1, hd], xr.at[i, 1, hd], left)

    def onward_right(i, hd):
        part = pl.ds(0, HALF)
        return remote(att.at[i, 3, hd, part], att.at[i, 2, hd, part], rs.at[i, 0, hd], rr.at[i, 0, hd], right)

    def onward_left(i, hd):
        part = pl.ds(HALF, HALF)
        return remote(att.at[i, 1, hd, part], att.at[i, 2, hd, part], rs.at[i, 1, hd], rr.at[i, 1, hd], left)

    def finish(i, hd):
        att[i, 0, hd] = (acc[i, hd, :, :HD] / acc[i, hd, :, HD:]).astype(BF16)
        to_right(i, hd).start()
        to_left(i, hd).start()

    def pass_on(i, hd):
        to_right(i, hd).wait_recv()
        onward_right(i, hd).start()
        to_left(i, hd).wait_recv()
        onward_left(i, hd).start()

    def to_z(i):
        return remote(pz.at[i], got.at[i], zs.at[i], zr.at[i], zpart)

    def project(i):
        each(lambda hd: onward_right(i, hd).wait_recv(), lambda hd: onward_left(i, hd).wait_recv())
        rows_of = jnp.concatenate([att[i, r, hd] for r in range(NX) for hd in range(NH)], axis=1)

        def block(g):
            weight = jnp.concatenate([wb[g, r] for r in range(NX)], axis=0)
            return jnp.dot(rows_of, weight, preferred_element_type=F32)

        pz[i] = block(0).astype(BF16)
        to_z(i).start()
        own[i] = block(1)

    def collect(i):
        to_z(i).wait_recv()
        o_ref[(core + i) % 2] = (own[i] + got[i].astype(F32)).astype(BF16)

    attend_both(3, 2, first=True)
    each(lambda hd: to_sib(4, hd).wait_recv())

    @pl.when(over_ok)
    def _():
        each(lambda hd: to_over(hd).start())

    each(lambda hd: to_sib(3, hd).wait_recv())
    attend_both(5, 2)

    @pl.when(far_ok)
    def _():
        each(lambda hd: to_far(hd).wait_recv(), lambda hd: forward(hd).start())
        each(lambda hd: to_far(hd).wait_send(), lambda hd: edge_values(hd).start())

    @pl.when(over_ok)
    def _():
        each(lambda hd: to_over(hd).wait_send(), lambda hd: edge_keys(hd).start())

    @pl.loop(0, NH)
    def _(hd):
        @pl.when(far_ok)
        def _():
            to_over(hd).wait_recv()
            attend(1, hd, 1, 2)

        @pl.when(over_ok)
        def _():
            forward(hd).wait_recv()
            attend(1, hd, 7, 1)

        finish(1, hd)

    for copy in w_out:
        copy.wait_recv()
    for copy in w_pass:
        copy.start()

    @pl.loop(0, NH)
    def _(hd):
        @pl.when(far_ok)
        def _():
            attend(0, hd, 1, 2)

        pass_on(1, hd)

    @pl.loop(0, NH)
    def _(hd):
        @pl.when(far_ok)
        def _():
            edge_keys(hd).wait_recv()
            edge_values(hd).wait_recv()
            attend(0, hd, 0, 1)

        finish(0, hd)

    for copy in w_in:
        copy.wait()
    for copy in w_pass:
        copy.wait_recv()
    project(1)
    each(lambda hd: pass_on(0, hd))
    project(0)
    collect(1)
    collect(0)

    each(lambda hd: to_sib(4, hd).wait_send(), lambda hd: to_sib(3, hd).wait_send())

    @pl.when(far_ok)
    def _():
        each(lambda hd: forward(hd).wait_send(), lambda hd: edge_values(hd).wait_send())

    @pl.when(over_ok)
    def _():
        each(lambda hd: edge_keys(hd).wait_send())

    for copy in w_out + w_pass:
        copy.wait_send()
    for i in range(2):
        each(
            lambda hd: to_right(i, hd).wait_send(),
            lambda hd: to_left(i, hd).wait_send(),
            lambda hd: onward_right(i, hd).wait_send(),
            lambda hd: onward_left(i, hd).wait_send(),
        )
        to_z(i).wait_send()


def body(query_tok, key_tok, value_tok, head_span, out_weight):
    anywhere = pl.BlockSpec(memory_space=pl.ANY)
    dma = pltpu.SemaphoreType.DMA
    out = pl.pallas_call(
        kernel,
        name="window_attention",
        out_shape=pltpu.VMEM((2, T, G), BF16),
        in_specs=[pl.BlockSpec(memory_space=pltpu.SMEM)] + [anywhere] * 4,
        out_specs=pl.BlockSpec(memory_space=pltpu.VMEM),
        scratch_shapes=[
            pltpu.VMEM((2, NH, T, HD), BF16),
            pltpu.VMEM((8, NH, 2, T, HD), BF16),
            pltpu.VMEM((2, NX, G, G), BF16),
            pltpu.VMEM((2, NH, T, 2 * HD), F32),
            pltpu.VMEM((2, NH, T, HD), F32),
            pltpu.VMEM((2, NX, NH, T, HD), BF16),
            pltpu.VMEM((2, T, G), BF16),
            pltpu.VMEM((2, T, G), F32),
            pltpu.VMEM((2, T, G), BF16),
            dma((20,)),
            dma((8, NH)),
            dma((8, NH)),
            dma((2, NH)),
            dma((2, NH)),
            dma((6, 2)),
            dma((6, 2)),
            dma((2, 2, NH)),
            dma((2, 2, NH)),
            dma((2, 2, NH)),
            dma((2, 2, NH)),
            dma((2,)),
            dma((2,)),
        ],
        compiler_params=pltpu.CompilerParams(
            collective_id=0, has_side_effects=True, vmem_limit_bytes=56 * 1024 * 1024
        ),
    )(head_span, query_tok, key_tok, value_tok, out_weight)
    return out.reshape(2 * T, G)


def solution(mesh):
    return jax.shard_map(
        body,
        mesh=mesh,
        in_specs=(
            P("frame", "head"),
            P("frame", "head"),
            P("frame", "head"),
            P("head"),
            P("head", None),
        ),
        out_specs=P("frame", "head"),
        check_vma=False,
    )
```

```python
import math

import jax
import jax.numpy as jnp
from jax import lax
from jax.experimental import pallas as pl
from jax.experimental.pallas import tpu as pltpu
from jax.sharding import PartitionSpec as P

MESH = pl.DeviceIdType.MESH
HD = 128
T = 384
HALF = T // 2
G = 384
NH = 3
NX = 4
F32 = jnp.float32
BF16 = jnp.bfloat16
SCALE = math.log2(math.e) / math.sqrt(HD)
HIDDEN = -1e30


def kernel(
    span_ref, q_hbm, k_hbm, v_hbm, w_hbm, o_ref,
    qv, kv, wb, acc, top, att, pz, part, got,
    lsem, hs, hr, es, er, ws, wr, xs, xr, rs, rr, zs, zr,
):
    head = lax.axis_index("head")
    frame = lax.axis_index("frame")
    frames = lax.axis_size("frame")
    zh, x = head // NX, head % NX
    core = frame % 2
    step = 1 - 2 * core
    sib = (head, frame + step)
    far = (head, frame - step)
    over = (head, frame + 2 * step)
    under = (head, frame - 2 * step)
    last = frames - 1
    far_ok = (frame - step >= 0) & (frame - step <= last)
    over_ok = (frame + 2 * step >= 0) & (frame + 2 * step <= last)
    zpart = ((1 - zh) * NX + x, frame)
    right = (zh * NX + (x + 1) % NX, frame)
    left = (zh * NX + (x + NX - 1) % NX, frame)
    across = (zh * NX + (x + 2) % NX, frame)

    def rows(i):
        return pl.ds(pl.multiple_of((core + i) % 2 * T, T), T)

    def columns(g, d):
        group = zh if g else 1 - zh
        return pl.ds(pl.multiple_of((group * NX + d) * G, G), G)

    def local(src, dst, n):
        copy = pltpu.make_async_copy(src, dst, lsem.at[n])
        copy.start()
        return copy

    def remote(src, dst, send, recv, device):
        return pltpu.make_async_remote_copy(
            src_ref=src, dst_ref=dst, send_sem=send, recv_sem=recv, device_id=device, device_id_type=MESH
        )

    own_in, n = [], 0
    for i in range(2):
        for hd in range(NH):
            cols = pl.ds(hd * HD, HD)
            own_in.append(local(k_hbm.at[rows(i), cols], kv.at[3 + i, hd, 0], n))
            own_in.append(local(v_hbm.at[rows(i), cols], kv.at[3 + i, hd, 1], n + 1))
            own_in.append(local(q_hbm.at[rows(i), cols], qv.at[i, hd], n + 2))
            n += 3
    w_in = [local(w_hbm.at[:, columns(g, x)], wb.at[g, 0], n + g) for g in range(2)]

    barrier = pltpu.get_barrier_semaphore()

    def greet(device):
        pl.semaphore_signal(barrier, inc=1, device_id=device, device_id_type=MESH)

    for device in (sib, zpart, right, left, across):
        greet(device)

    @pl.when(far_ok)
    def _():
        greet(far)
        greet(under)

    @pl.when(over_ok)
    def _():
        greet(over)

    for copy in own_in:
        copy.wait()
    pl.semaphore_wait(barrier, 5 + 2 * far_ok.astype(jnp.int32) + over_ok.astype(jnp.int32))

    def halo(src, dst, device, hd):
        return remote(kv.at[src, hd], kv.at[dst, hd], hs.at[dst, hd], hr.at[dst, hd], device)

    def to_far(hd):
        return halo(3, 2, far, hd)

    def to_sib(src, hd):
        return halo(src, 9 - src, sib, hd)

    def to_over(hd):
        return halo(5, 1, over, hd)

    def forward(hd):
        return halo(2, 7, sib, hd)

    def edge_keys(hd):
        return remote(kv.at[4, hd, 0], kv.at[0, hd, 0], es.at[0, hd], er.at[0, hd], over)

    def edge_values(hd):
        return remote(kv.at[5, hd, 1], kv.at[0, hd, 1], es.at[1, hd], er.at[1, hd], far)

    def each(*actions):
        @pl.loop(0, NH)
        def _(hd):
            for action in actions:
                action(hd)

    @pl.when(far_ok)
    def _():
        to_far(0).start()

    each(lambda hd: to_sib(4, hd).start(), lambda hd: to_sib(3, hd).start())

    mine = pl.ds(pl.multiple_of(core * HALF, HALF), HALF)
    w_out = [
        remote(w_hbm.at[mine, columns(g, (x + r) % NX)], wb.at[g, NX - r, mine, :], ws.at[r - 1, g], wr.at[r - 1, g], device)
        for r, device in ((2, across), (1, right), (3, left))
        for g in range(2)
    ]
    w_pass = [
        remote(wb.at[:, r, mine, :], wb.at[:, r, mine, :], ws.at[NX - 2 + r, 0], wr.at[NX - 2 + r, 0], sib)
        for r in range(1, NX)
    ]
    for copy in w_out:
        copy.start()

    def attend(i, hd, slot, n, first=False):
        keys = kv[slot : slot + n, hd, 0].reshape(n * T, HD)
        values = kv[slot : slot + n, hd, 1].reshape(n * T, HD)
        s = lax.dot_general(qv[i, hd], keys, (((1,), (1,)), ((), ())), preferred_element_type=F32) * SCALE
        span = span_ref[hd]
        bias = [jnp.where(jnp.abs(3 + i - slot - m) <= span, 0.0, HIDDEN).astype(F32) for m in range(n)]
        new = None
        for m in range(n):
            peak = jnp.max(s[:, m * T : (m + 1) * T], axis=1, keepdims=True) + bias[m]
            new = peak if new is None else jnp.maximum(new, peak)
        new = jnp.broadcast_to(new, (T, HD))
        if not first:
            old = top[i, hd]
            new = jnp.maximum(old, new)
            shrink = jnp.exp2(old - new)
        shift = jnp.concatenate([new - b for b in bias for _ in range(T // HD)], axis=1)
        p = jnp.exp2(s - shift).astype(BF16)
        extended = jnp.concatenate([values, jnp.ones((n * T, HD), BF16)], axis=1)
        out = jnp.dot(p, extended, preferred_element_type=F32)
        top[i, hd] = new
        if first:
            acc[i, hd] = out
        else:
            acc[i, hd] = acc[i, hd] * jnp.concatenate([shrink, shrink], axis=1) + out

    def piece(i, source, k, part=None):
        if i:
            ref = att.at[i, source, k]
            return ref if part is None else ref.at[pl.ds(part * HALF, HALF)]
        if part is None:
            return att.at[i, source, :, pl.ds(k * HALF, HALF)]
        return att.at[i, source, :, pl.ds(k * HALF + part * (HALF // 2), HALF // 2)]

    def to_right(i, k):
        return remote(piece(i, 0, k), piece(i, 3, k), xs.at[i, 0, k], xr.at[i, 0, k], right)

    def to_left(i, k):
        return remote(piece(i, 0, k), piece(i, 1, k), xs.at[i, 1, k], xr.at[i, 1, k], left)

    def onward_right(i, k):
        return remote(piece(i, 3, k, 0), piece(i, 2, k, 0), rs.at[i, 0, k], rr.at[i, 0, k], right)

    def onward_left(i, k):
        return remote(piece(i, 1, k, 1), piece(i, 2, k, 1), rs.at[i, 1, k], rr.at[i, 1, k], left)

    def finish(i, hd):
        att[i, 0, hd] = (acc[i, hd, :, :HD] / acc[i, hd, :, HD:]).astype(BF16)

    def send_x(i, k):
        to_right(i, k).start()
        to_left(i, k).start()

    def pass_on(i, k):
        to_right(i, k).wait_recv()
        onward_right(i, k).start()
        to_left(i, k).wait_recv()
        onward_left(i, k).start()

    def gathered_x(i, k):
        onward_right(i, k).wait_recv()
        onward_left(i, k).wait_recv()

    def to_z(i, k, size):
        where = pl.ds(k * size, size)
        return remote(pz.at[i, where], got.at[i, where], zs.at[2 * i + k], zr.at[2 * i + k], zpart)

    def project(i, k, size):
        where = slice(k * size, (k + 1) * size)
        gathered = jnp.concatenate([att[i, r, hd, where] for r in range(NX) for hd in range(NH)], axis=1)

        def columns_of(g):
            weight = jnp.concatenate([wb[g, r] for r in range(NX)], axis=0)
            return jnp.dot(gathered, weight, preferred_element_type=F32)

        pz[i, where] = columns_of(0).astype(BF16)
        to_z(i, k, size).start()
        part[i, where] = columns_of(1)

    def collect(i, k, size):
        to_z(i, k, size).wait_recv()
        where = slice(k * size, (k + 1) * size)
        o_ref[(core + i) % 2, where] = (part[i, where] + got[i, where].astype(F32)).astype(BF16)

    @pl.loop(0, NH + 1)
    def _(step_no):
        hd = step_no
        before = step_no - 1

        @pl.when(far_ok & (step_no > 0))
        def _():
            to_far(before).wait_recv()
            forward(before).start()

        @pl.when(step_no < NH)
        def _():
            to_sib(4, hd).wait_recv()

            @pl.when(over_ok)
            def _():
                to_over(hd).start()

            @pl.when(far_ok & (hd < NH - 1))
            def _():
                to_far(hd + 1).start()

            to_sib(3, hd).wait_recv()
            for i in range(2):
                attend(i, hd, 3, 4, first=True)

        @pl.when(step_no == NH - 1)
        def _():
            @pl.when(far_ok)
            def _():
                each(lambda hd: edge_values(hd).start())

            @pl.when(over_ok)
            def _():
                each(lambda hd: edge_keys(hd).start())

        @pl.when(step_no > 0)
        def _():
            @pl.when(far_ok)
            def _():
                to_over(before).wait_recv()
                attend(1, before, 1, 2)

            @pl.when(over_ok)
            def _():
                forward(before).wait_recv()
                attend(1, before, 7, 1)

            finish(1, before)
            send_x(1, before)

    for copy in w_out:
        copy.wait_recv()
    for copy in w_pass:
        copy.start()

    @pl.loop(0, NH)
    def _(hd):
        @pl.when(far_ok)
        def _():
            attend(0, hd, 1, 2)

        pass_on(1, hd)

    @pl.loop(0, NH)
    def _(hd):
        @pl.when(far_ok)
        def _():
            edge_keys(hd).wait_recv()
            edge_values(hd).wait_recv()
            attend(0, hd, 0, 1)

        finish(0, hd)

    send_x(0, 0)
    send_x(0, 1)
    for copy in w_in:
        copy.wait()
    for copy in w_pass:
        copy.wait_recv()
    each(lambda hd: gathered_x(1, hd))
    project(1, 0, T)
    pass_on(0, 0)
    pass_on(0, 1)
    for k in range(2):
        gathered_x(0, k)
        project(0, k, HALF)
    collect(1, 0, T)
    for k in range(2):
        collect(0, k, HALF)

    each(lambda hd: to_sib(4, hd).wait_send(), lambda hd: to_sib(3, hd).wait_send())

    @pl.when(far_ok)
    def _():
        each(
            lambda hd: to_far(hd).wait_send(),
            lambda hd: forward(hd).wait_send(),
            lambda hd: edge_values(hd).wait_send(),
        )

    @pl.when(over_ok)
    def _():
        each(lambda hd: to_over(hd).wait_send(), lambda hd: edge_keys(hd).wait_send())

    for copy in w_out + w_pass:
        copy.wait_send()
    for i, pieces in ((1, NH), (0, 2)):
        for k in range(pieces):
            for move in (to_right, to_left, onward_right, onward_left):
                move(i, k).wait_send()
    to_z(1, 0, T).wait_send()
    for k in range(2):
        to_z(0, k, HALF).wait_send()


def body(query_tok, key_tok, value_tok, head_span, out_weight):
    anywhere = pl.BlockSpec(memory_space=pl.ANY)
    dma = pltpu.SemaphoreType.DMA
    out = pl.pallas_call(
        kernel,
        name="window_attention",
        out_shape=pltpu.VMEM((2, T, G), BF16),
        in_specs=[pl.BlockSpec(memory_space=pltpu.SMEM)] + [anywhere] * 4,
        out_specs=pl.BlockSpec(memory_space=pltpu.VMEM),
        scratch_shapes=[
            pltpu.VMEM((2, NH, T, HD), BF16),
            pltpu.VMEM((8, NH, 2, T, HD), BF16),
            pltpu.VMEM((2, NX, G, G), BF16),
            pltpu.VMEM((2, NH, T, 2 * HD), F32),
            pltpu.VMEM((2, NH, T, HD), F32),
            pltpu.VMEM((2, NX, NH, T, HD), BF16),
            pltpu.VMEM((2, T, G), BF16),
            pltpu.VMEM((2, T, G), F32),
            pltpu.VMEM((2, T, G), BF16),
            dma((20,)),
            dma((8, NH)),
            dma((8, NH)),
            dma((2, NH)),
            dma((2, NH)),
            dma((6, 2)),
            dma((6, 2)),
            dma((2, 2, NH)),
            dma((2, 2, NH)),
            dma((2, 2, NH)),
            dma((2, 2, NH)),
            dma((3,)),
            dma((3,)),
        ],
        compiler_params=pltpu.CompilerParams(
            collective_id=0, has_side_effects=True, vmem_limit_bytes=56 * 1024 * 1024
        ),
    )(head_span, query_tok, key_tok, value_tok, out_weight)
    return out.reshape(2 * T, G)


def solution(mesh):
    return jax.shard_map(
        body,
        mesh=mesh,
        in_specs=(
            P("frame", "head"),
            P("frame", "head"),
            P("frame", "head"),
            P("head"),
            P("head", None),
        ),
        out_specs=P("frame", "head"),
        check_vma=False,
    )
```

```python
import math

import jax
import jax.numpy as jnp
from jax import lax
from jax.experimental import pallas as pl
from jax.experimental.pallas import tpu as pltpu
from jax.sharding import PartitionSpec as P

MESH = pl.DeviceIdType.MESH
HD = 128
T = 384
HALF = T // 2
PIECES = 3
PIECE = T // PIECES
G = 384
NH = 3
NX = 4
F32 = jnp.float32
BF16 = jnp.bfloat16
SCALE = math.log2(math.e) / math.sqrt(HD)
HIDDEN = -1e30


def kernel(
    span_ref, q_hbm, k_hbm, v_hbm, w_hbm, o_ref,
    qv, kv, wb, acc, top, att, pz, part, got,
    lsem, hs, hr, es, er, ws, wr, xs, xr, rs, rr, zs, zr,
):
    head = lax.axis_index("head")
    frame = lax.axis_index("frame")
    frames = lax.axis_size("frame")
    zh, x = head // NX, head % NX
    core = frame % 2
    step = 1 - 2 * core
    sib = (head, frame + step)
    far = (head, frame - step)
    over = (head, frame + 2 * step)
    under = (head, frame - 2 * step)
    last = frames - 1
    far_ok = (frame - step >= 0) & (frame - step <= last)
    over_ok = (frame + 2 * step >= 0) & (frame + 2 * step <= last)
    zpart = ((1 - zh) * NX + x, frame)
    right = (zh * NX + (x + 1) % NX, frame)
    left = (zh * NX + (x + NX - 1) % NX, frame)
    across = (zh * NX + (x + 2) % NX, frame)

    def rows(i):
        return pl.ds(pl.multiple_of((core + i) % 2 * T, T), T)

    def columns(g, d):
        group = zh if g else 1 - zh
        return pl.ds(pl.multiple_of((group * NX + d) * G, G), G)

    def local(src, dst, n):
        copy = pltpu.make_async_copy(src, dst, lsem.at[n])
        copy.start()
        return copy

    def remote(src, dst, send, recv, device):
        return pltpu.make_async_remote_copy(
            src_ref=src, dst_ref=dst, send_sem=send, recv_sem=recv, device_id=device, device_id_type=MESH
        )

    barrier = pltpu.get_barrier_semaphore()

    def greet(device):
        pl.semaphore_signal(barrier, inc=1, device_id=device, device_id_type=MESH)

    for device in (sib, zpart, right, left, across):
        greet(device)

    @pl.when(far_ok)
    def _():
        greet(far)
        greet(under)

    @pl.when(over_ok)
    def _():
        greet(over)

    own_in, n = [], 0
    for i in range(2):
        for hd in range(NH):
            cols = pl.ds(hd * HD, HD)
            own_in.append(local(k_hbm.at[rows(i), cols], kv.at[3 + i, hd, 0], n))
            own_in.append(local(v_hbm.at[rows(i), cols], kv.at[3 + i, hd, 1], n + 1))
            own_in.append(local(q_hbm.at[rows(i), cols], qv.at[i, hd], n + 2))
            n += 3
    w_in = [local(w_hbm.at[:, columns(g, x)], wb.at[g, 0], n + g) for g in range(2)]

    for copy in own_in:
        copy.wait()
    pl.semaphore_wait(barrier, 5 + 2 * far_ok.astype(jnp.int32) + over_ok.astype(jnp.int32))

    def halo(src, dst, device, hd):
        return remote(kv.at[src, hd], kv.at[dst, hd], hs.at[dst, hd], hr.at[dst, hd], device)

    def to_far(hd):
        return halo(3, 2, far, hd)

    def to_sib(src, hd):
        return halo(src, 9 - src, sib, hd)

    def to_over(hd):
        return halo(5, 1, over, hd)

    def forward(hd):
        return halo(2, 7, sib, hd)

    def edge_keys(hd):
        return remote(kv.at[4, hd, 0], kv.at[0, hd, 0], es.at[0, hd], er.at[0, hd], over)

    def edge_values(hd):
        return remote(kv.at[5, hd, 1], kv.at[0, hd, 1], es.at[1, hd], er.at[1, hd], far)

    def each(*actions):
        @pl.loop(0, NH)
        def _(hd):
            for action in actions:
                action(hd)

    @pl.when(far_ok)
    def _():
        to_far(0).start()

    each(lambda hd: to_sib(4, hd).start(), lambda hd: to_sib(3, hd).start())

    mine = pl.ds(pl.multiple_of(core * HALF, HALF), HALF)
    w_out = [
        remote(w_hbm.at[mine, columns(g, (x + r) % NX)], wb.at[g, NX - r, mine, :], ws.at[r - 1, g], wr.at[r - 1, g], device)
        for r, device in ((2, across), (1, right), (3, left))
        for g in range(2)
    ]
    w_pass = [
        remote(wb.at[:, r, mine, :], wb.at[:, r, mine, :], ws.at[NX - 2 + r, 0], wr.at[NX - 2 + r, 0], sib)
        for r in range(1, NX)
    ]
    for copy in w_out:
        copy.start()

    def attend(i, hd, slot, n, first=False):
        keys = kv[slot : slot + n, hd, 0].reshape(n * T, HD)
        values = kv[slot : slot + n, hd, 1].reshape(n * T, HD)
        s = lax.dot_general(qv[i, hd], keys, (((1,), (1,)), ((), ())), preferred_element_type=F32) * SCALE
        span = span_ref[hd]
        bias = [jnp.where(jnp.abs(3 + i - slot - m) <= span, 0.0, HIDDEN).astype(F32) for m in range(n)]
        new = None
        for m in range(n):
            peak = jnp.max(s[:, m * T : (m + 1) * T], axis=1, keepdims=True) + bias[m]
            new = peak if new is None else jnp.maximum(new, peak)
        new = jnp.broadcast_to(new, (T, HD))
        if not first:
            old = top[i, hd]
            new = jnp.maximum(old, new)
            shrink = jnp.exp2(old - new)
        shift = jnp.concatenate([new - b for b in bias for _ in range(T // HD)], axis=1)
        p = jnp.exp2(s - shift).astype(BF16)
        extended = jnp.concatenate([values, jnp.ones((n * T, HD), BF16)], axis=1)
        out = jnp.dot(p, extended, preferred_element_type=F32)
        top[i, hd] = new
        if first:
            acc[i, hd] = out
        else:
            acc[i, hd] = acc[i, hd] * jnp.concatenate([shrink, shrink], axis=1) + out

    def piece(i, source, k, part=None):
        if i:
            ref = att.at[i, source, k]
            return ref if part is None else ref.at[pl.ds(part * HALF, HALF)]
        if part is None:
            return att.at[i, source, :, pl.ds(k * PIECE, PIECE)]
        return att.at[i, source, :, pl.ds(k * PIECE + part * (PIECE // 2), PIECE // 2)]

    def to_right(i, k):
        return remote(piece(i, 0, k), piece(i, 3, k), xs.at[i, 0, k], xr.at[i, 0, k], right)

    def to_left(i, k):
        return remote(piece(i, 0, k), piece(i, 1, k), xs.at[i, 1, k], xr.at[i, 1, k], left)

    def onward_right(i, k):
        return remote(piece(i, 3, k, 0), piece(i, 2, k, 0), rs.at[i, 0, k], rr.at[i, 0, k], right)

    def onward_left(i, k):
        return remote(piece(i, 1, k, 1), piece(i, 2, k, 1), rs.at[i, 1, k], rr.at[i, 1, k], left)

    def finish(i, hd):
        att[i, 0, hd] = (acc[i, hd, :, :HD] / acc[i, hd, :, HD:]).astype(BF16)

    def send_x(i, k):
        to_right(i, k).start()
        to_left(i, k).start()

    def pass_on(i, k):
        to_right(i, k).wait_recv()
        onward_right(i, k).start()
        to_left(i, k).wait_recv()
        onward_left(i, k).start()

    def gathered_x(i, k):
        onward_right(i, k).wait_recv()
        onward_left(i, k).wait_recv()

    def to_z(i, k, size):
        where = pl.ds(k * size, size)
        return remote(pz.at[i, where], got.at[i, where], zs.at[PIECES * i + k], zr.at[PIECES * i + k], zpart)

    def project(i, k, size):
        where = slice(k * size, (k + 1) * size)
        gathered = jnp.concatenate([att[i, r, hd, where] for r in range(NX) for hd in range(NH)], axis=1)

        def columns_of(g):
            weight = jnp.concatenate([wb[g, r] for r in range(NX)], axis=0)
            return jnp.dot(gathered, weight, preferred_element_type=F32)

        pz[i, where] = columns_of(0).astype(BF16)
        to_z(i, k, size).start()
        part[i, where] = columns_of(1)

    def collect(i, k, size):
        to_z(i, k, size).wait_recv()
        where = slice(k * size, (k + 1) * size)
        o_ref[(core + i) % 2, where] = (part[i, where] + got[i, where].astype(F32)).astype(BF16)

    @pl.loop(0, NH + 1)
    def _(step_no):
        hd = step_no
        before = step_no - 1

        @pl.when(far_ok & (step_no > 0))
        def _():
            to_far(before).wait_recv()
            forward(before).start()

        @pl.when(step_no < NH)
        def _():
            to_sib(4, hd).wait_recv()

            @pl.when(over_ok)
            def _():
                to_over(hd).start()

            @pl.when(far_ok & (hd < NH - 1))
            def _():
                to_far(hd + 1).start()

            to_sib(3, hd).wait_recv()
            for i in range(2):
                attend(i, hd, 3, 4, first=True)

        @pl.when(step_no == NH)
        def _():
            @pl.when(far_ok)
            def _():
                each(lambda hd: edge_values(hd).start())

            @pl.when(over_ok)
            def _():
                each(lambda hd: edge_keys(hd).start())

        @pl.when(step_no == NH)
        def _():
            pass_on(1, 0)

        @pl.when(step_no > 0)
        def _():
            @pl.when(far_ok)
            def _():
                to_over(before).wait_recv()
                attend(1, before, 1, 2)

            @pl.when(over_ok)
            def _():
                forward(before).wait_recv()
                attend(1, before, 7, 1)

            finish(1, before)
            send_x(1, before)

    pass_on(1, 1)
    for copy in w_out:
        copy.wait_recv()
    for copy in w_pass:
        copy.start()

    @pl.when(far_ok)
    def _():
        for hd in range(NH):
            attend(0, hd, 1, 2)

    pass_on(1, NH - 1)

    @pl.when(far_ok)
    def _():
        each(lambda hd: edge_keys(hd).wait_recv(), lambda hd: edge_values(hd).wait_recv())
        for hd in range(NH):
            attend(0, hd, 0, 1)

    for hd in range(NH):
        finish(0, hd)

    for k in range(PIECES):
        send_x(0, k)
    for copy in w_in:
        copy.wait()
    for copy in w_pass:
        copy.wait_recv()
    each(lambda hd: gathered_x(1, hd))
    project(1, 0, T)
    for k in range(PIECES):
        pass_on(0, k)
    for k in range(PIECES):
        gathered_x(0, k)
        project(0, k, PIECE)
    collect(1, 0, T)
    for k in range(PIECES):
        collect(0, k, PIECE)

    each(lambda hd: to_sib(4, hd).wait_send(), lambda hd: to_sib(3, hd).wait_send())

    @pl.when(far_ok)
    def _():
        each(
            lambda hd: to_far(hd).wait_send(),
            lambda hd: forward(hd).wait_send(),
            lambda hd: edge_values(hd).wait_send(),
        )

    @pl.when(over_ok)
    def _():
        each(lambda hd: to_over(hd).wait_send(), lambda hd: edge_keys(hd).wait_send())

    for copy in w_out + w_pass:
        copy.wait_send()
    for i, pieces in ((1, NH), (0, PIECES)):
        for k in range(pieces):
            for move in (to_right, to_left, onward_right, onward_left):
                move(i, k).wait_send()
    to_z(1, 0, T).wait_send()
    for k in range(PIECES):
        to_z(0, k, PIECE).wait_send()


def body(query_tok, key_tok, value_tok, head_span, out_weight):
    anywhere = pl.BlockSpec(memory_space=pl.ANY)
    dma = pltpu.SemaphoreType.DMA
    out = pl.pallas_call(
        kernel,
        name="window_attention",
        out_shape=pltpu.VMEM((2, T, G), BF16),
        in_specs=[pl.BlockSpec(memory_space=pltpu.SMEM)] + [anywhere] * 4,
        out_specs=pl.BlockSpec(memory_space=pltpu.VMEM),
        scratch_shapes=[
            pltpu.VMEM((2, NH, T, HD), BF16),
            pltpu.VMEM((8, NH, 2, T, HD), BF16),
            pltpu.VMEM((2, NX, G, G), BF16),
            pltpu.VMEM((2, NH, T, 2 * HD), F32),
            pltpu.VMEM((2, NH, T, HD), F32),
            pltpu.VMEM((2, NX, NH, T, HD), BF16),
            pltpu.VMEM((2, T, G), BF16),
            pltpu.VMEM((2, T, G), F32),
            pltpu.VMEM((2, T, G), BF16),
            dma((20,)),
            dma((8, NH)),
            dma((8, NH)),
            dma((2, NH)),
            dma((2, NH)),
            dma((6, 2)),
            dma((6, 2)),
            dma((2, 2, NH)),
            dma((2, 2, NH)),
            dma((2, 2, NH)),
            dma((2, 2, NH)),
            dma((PIECES + 1,)),
            dma((PIECES + 1,)),
        ],
        compiler_params=pltpu.CompilerParams(
            collective_id=0, has_side_effects=True, vmem_limit_bytes=56 * 1024 * 1024
        ),
    )(head_span, query_tok, key_tok, value_tok, out_weight)
    return out.reshape(2 * T, G)


def solution(mesh):
    return jax.shard_map(
        body,
        mesh=mesh,
        in_specs=(
            P("frame", "head"),
            P("frame", "head"),
            P("frame", "head"),
            P("head"),
            P("head", None),
        ),
        out_specs=P("frame", "head"),
        check_vma=False,
    )
```
